128 devices in a mesh: kv: 32 (over y, z, x_hi), pb: 4 (over x_lo, core).
Axes of the slice: x: 4 (x_hi: 2, x_lo: 2; x = x_hi * 2 + x_lo), y: 4, z: 4, core: 2. Of those that a mesh axis runs over, the one named last changes fastest.
Arguments:
- queries: bfloat16 [49152, 4096], P('kv', 'pb'), may hold values from -12 to 12
- cached_keys: bfloat16 [32, 256, 4096], P('kv', None, 'pb'), may hold values from -6 to 6
- cached_values: bfloat16 [32, 256, 4096], P('kv', None, 'pb'), may hold values from -6 to 6
- block_map: int32 [768, 1], P('kv'), may hold values from 0 to 31; in each aligned block of 24 rows (0 to 23, 24 to 47, ...) at most 2 rows name the same one
- out_weight: bfloat16 [4096, 4096], P('pb'), may hold values from -0.09375 to 0.09375
- hidden: bfloat16 [49152, 4096], P('kv', 'pb'), may hold values from -6 to 6
Outputs:
- mixed: bfloat16 [49152, 4096], P('kv', 'pb')
The draws below stay inside these ranges and needn't reach their ends.
Inputs may be any that keep to these rules, and one draw needn't show every extreme that they name: `block_map`: at most 2 of the 24 spans of one index of kv name the same block, and some index has a block named by exactly 2 of its spans; every block is named by some span.
All inputs are finite; a program needn't handle non-finite values.
Results may differ from the reference program's by a relative error of at most 0.0085.
Values may be sent and summed in bfloat16 or wider, within the bound.
No kernel may reach another device: no remote copies, remote signals or barrier semaphores. Data moves between devices by JAX's collectives and lax.ppermute only.
A program may use at most 192 MiB of HBM per device.

```python
import math
import jax
import jax.numpy as jnp
import numpy as np
from jax import lax

D = 4096
HEADS = 32
HEAD = 128
SPAN = 64
CH_DEV = 24
CAP = 2
KEYS = 256
BLOCKS = 32
SPANS = 768
TOKENS = 49152
N_PB = 4


def draw_queries(key, part):
    base_key = jax.random.fold_in(key, 11)
    values = jnp.clip(jax.random.normal(jax.random.fold_in(base_key, 2), (TOKENS, D)), -6.0, 6.0)
    return values.astype(jnp.float32).astype(jnp.bfloat16)


def draw_cached_keys(key, part):
    base_key = jax.random.fold_in(key, 23)
    values = jnp.clip(jax.random.normal(jax.random.fold_in(base_key, 2), (BLOCKS, KEYS, D)), -6.0, 6.0)
    return values.astype(jnp.float32).astype(jnp.bfloat16)


def shard_levels(rng, extent, shards, least, top_value):
    level = 1.0
    for position, blocks in shards:
        steps = jax.random.uniform(jax.random.fold_in(jax.random.fold_in(rng, 6), position), (blocks,), jnp.float32, least / len(shards), top_value / len(shards))
        level = level * jnp.repeat(jnp.exp(steps), extent[position] // blocks).reshape((-1,) + (1,) * (len(extent) - 1 - position))
    return level


def deal_out(own_key, own, number, rows, number_of, top, most, slope):
    order = jax.random.permutation(own_key, number_of)
    heavy_load, common = load_shares(number_of, rows * top, most, slope, True), load_shares(number_of, rows * top, most, slope, False)
    places = jnp.arange(number_of)

    def named(sizes, offset_by):
        used = int((sizes > 0).sum())
        fixed = max(1, used // 4)
        moved = fixed + (places - fixed + offset_by * (used - fixed)) % max(1, number_of - fixed)
        return jnp.zeros((number_of,), jnp.int32).at[order[jnp.where(places < fixed, places, moved)]].set(jnp.asarray(sizes, jnp.int32))

    sizes = jnp.where(number % 4 == 0, named(heavy_load, number // 4), named(common, number - number // 4 - 1))
    mixed = jax.random.permutation(jax.random.fold_in(own, 3), number_of)
    giver, sink = mixed[0:number_of // 2 * 2:2], mixed[1:number_of // 2 * 2:2]
    slack = jnp.minimum(sizes[giver] - 1, most - sizes[sink]) // 2
    slack = jnp.where((giver == order[0]) | (sink == order[0]) | (sizes[sink] == 0), 0, jnp.maximum(slack, 0))
    moved = jax.random.randint(jax.random.fold_in(own, 4), (number_of // 2,), 0, 1 << 20) % (slack + 1)
    sizes = sizes.at[giver].add(-moved).at[sink].add(moved)
    members = jnp.searchsorted(jnp.cumsum(sizes), jnp.arange(rows * top), side="right").astype(jnp.int32)
    grid = members.reshape(top, rows).T
    grid = grid[jax.random.permutation(jax.random.fold_in(own, 1), rows)]
    offset_by = jax.random.randint(jax.random.fold_in(own, 2), (rows, 1), 0, top)
    return jnp.take_along_axis(grid, (jnp.arange(top)[None, :] + offset_by) % top, axis=1)


def load_shares(amount, total, most, lean, full):
    weights = [(1 << 20) // math.isqrt(grade ** lean) + 1 for grade in range(1, amount + 1)]
    largest = most if full else min(most, max(-(-total // amount), total * weights[0] // sum(weights)))
    least = 1 if total - largest >= amount - 1 else 0
    holding, surplus = [largest] + [least] * (amount - 1), total - largest - least * (amount - 1)
    while surplus > 0:
        free = [i for i in range(1, amount) if holding[i] < largest] or [i for i in range(1, amount) if holding[i] < most]
        pool, remaining = sum([weights[i] for i in free]), surplus
        for i in free:
            more = min(most - holding[i], max(1, remaining * weights[i] // pool), surplus)
            holding[i] = holding[i] + more
            surplus = surplus - more
    return np.array(holding)


def scatter_about(key, shape, width, most, split=(), held_as=jnp.bfloat16):
    factor_of = shard_levels(key, shape, split, -0.22, 0.18) if split else 1.0
    entries = jax.random.normal(key, shape, jnp.float32) * width * factor_of
    return jnp.minimum(jnp.maximum(entries, -most), most).astype(held_as)


def setup_inputs(seed: int = 0) -> dict:
    seeds = jax.random.split(jax.random.key(seed), 7)
    queries = draw_queries(jax.random.fold_in(seeds[6], 71), 0)
    cached_keys = draw_cached_keys(jax.random.fold_in(seeds[6], 71), 0)
    cached_values = scatter_about(seeds[2], (BLOCKS, KEYS, D), 1.0, 6.0, ((0, 32), (2, 4)))
    block_map_keys = jax.random.split(jax.random.fold_in(seeds[3], 1), SPANS // CH_DEV)
    block_map_turns = jax.random.permutation(jax.random.fold_in(seeds[3], 3), SPANS // CH_DEV)
    block_map = jax.vmap(lambda own, number: deal_out(jax.random.fold_in(seeds[3], 2), own, number, CH_DEV, BLOCKS, 1, CAP, 2))(block_map_keys, block_map_turns).reshape((SPANS, 1))
    out_weight = scatter_about(seeds[4], (D, D), D ** -0.5, 0.09375, ((0, 4),))
    hidden = scatter_about(seeds[5], (TOKENS, D), 1.0, 6.0, ((0, 32), (1, 4)))
    return {"queries": queries, "cached_keys": cached_keys, "cached_values": cached_values, "block_map": block_map, "out_weight": out_weight, "hidden": hidden}


def reference(queries, cached_keys, cached_values, block_map, out_weight, hidden):
    targets = block_map[:, 0].astype(jnp.int32)
    q_spans = queries.reshape(SPANS, SPAN, HEADS, HEAD)

    def one_span(inputs):
        span_rows, target = inputs
        keys_now = lax.dynamic_index_in_dim(cached_keys, target, 0, keepdims=False)
        values_now = lax.dynamic_index_in_dim(cached_values, target, 0, keepdims=False)
        keys_now = keys_now.astype(jnp.float32).reshape(KEYS, HEADS, HEAD)
        values_now = values_now.astype(jnp.float32).reshape(KEYS, HEADS, HEAD)
        scores = jnp.einsum('rhd,khd->hrk', span_rows.astype(jnp.float32), keys_now) * (HEAD ** -0.5)
        row_top = jnp.max(scores, axis=-1, keepdims=True)
        exponent = jnp.exp(scores - row_top)
        weights = lax.optimization_barrier((exponent / jnp.sum(exponent, axis=-1, keepdims=True)).astype(jnp.bfloat16))
        result = jnp.einsum('hrk,khd->rhd', weights.astype(jnp.float32), values_now)
        return result.astype(jnp.bfloat16).reshape(SPAN, D)

    attended = lax.map(one_span, (q_spans, targets)).reshape(TOKENS, D)
    group_width = D // N_PB
    summed = jnp.zeros((TOKENS, D), jnp.float32)
    for head_group in range(N_PB):
        lower = head_group * group_width
        partial_value = jnp.dot(attended[:, lower:lower + group_width], out_weight[lower:lower + group_width], preferred_element_type=jnp.float32)
        partial_value = lax.optimization_barrier(partial_value.astype(jnp.bfloat16))
        summed = summed + partial_value.astype(jnp.float32)
    return (hidden.astype(jnp.float32) + summed).astype(jnp.bfloat16)
```

```python
import functools

import jax
import jax.numpy as jnp
from jax import lax
from jax.experimental import pallas as pl
from jax.experimental.pallas import tpu as pltpu
from jax.sharding import PartitionSpec as P

HEAD = 128
SPAN = 64
LOG2E = 1.4426950408889634


def attend_kernel(map_ref, q_ref, k_ref, v_ref, o_ref):
    head_count = q_ref.shape[-1] // HEAD
    scale = LOG2E * HEAD ** (-0.5)
    for head in range(head_count):
        cols = slice(head * HEAD, (head + 1) * HEAD)
        scores = lax.dot_general(
            q_ref[:, cols],
            k_ref[0, :, cols],
            (((1,), (1,)), ((), ())),
            preferred_element_type=jnp.float32,
        )
        row_top = jnp.max(scores, axis=-1, keepdims=True)
        exponent = jnp.exp2((scores - row_top) * scale)
        total = jnp.sum(exponent, axis=-1, keepdims=True)
        result = jnp.dot(
            exponent.astype(jnp.bfloat16), v_ref[0, :, cols], preferred_element_type=jnp.float32
        )
        o_ref[:, cols] = (result / total).astype(jnp.bfloat16)


def attend(queries, keys, values, targets):
    tok_rows, feat_width = queries.shape
    key_count = keys.shape[1]
    span_count = tok_rows // SPAN
    return pl.pallas_call(
        attend_kernel,
        out_shape=jax.ShapeDtypeStruct((tok_rows, feat_width), jnp.bfloat16),
        grid_spec=pltpu.PrefetchScalarGridSpec(
            num_scalar_prefetch=1,
            grid=(span_count,),
            in_specs=[
                pl.BlockSpec((SPAN, feat_width), lambda i, m: (i, 0)),
                pl.BlockSpec((1, key_count, feat_width), lambda i, m: (m[i], 0, 0)),
                pl.BlockSpec((1, key_count, feat_width), lambda i, m: (m[i], 0, 0)),
            ],
            out_specs=pl.BlockSpec((SPAN, feat_width), lambda i, m: (i, 0)),
        ),
        name="attend",
    )(targets, queries, keys, values)


def on_device(queries, cached_keys, cached_values, block_map, out_weight, hidden):
    targets = block_map[:, 0]
    key_piece = lax.all_gather(cached_keys, "kv", axis=0, tiled=True)
    value_piece = lax.all_gather(cached_values, "kv", axis=0, tiled=True)
    attended = attend(queries, key_piece, value_piece, targets)
    partial_value = jnp.dot(attended, out_weight, preferred_element_type=jnp.float32)
    summed = lax.psum_scatter(
        partial_value.astype(jnp.bfloat16), "pb", scatter_dimension=1, tiled=True
    ).astype(jnp.float32)
    return (hidden.astype(jnp.float32) + summed).astype(jnp.bfloat16)


def solution(mesh):
    placed = (
        P("kv", "pb"),
        P("kv", None, "pb"),
        P("kv", None, "pb"),
        P("kv", None),
        P("pb", None),
        P("kv", "pb"),
    )
    return jax.shard_map(
        on_device, mesh=mesh, in_specs=placed, out_specs=P("kv", "pb"), check_vma=False
    )
```

```python
import jax
import jax.numpy as jnp
from jax import lax
from jax.experimental import pallas as pl
from jax.experimental.pallas import tpu as pltpu
from jax.sharding import PartitionSpec as P

HEAD = 128
SPAN = 64
LOG2E = 1.4426950408889634
SIDE = 4
GROUPS = 4


def kv_index(y, z, half):
    return ((y % SIDE) * SIDE + z % SIDE) * 2 + half


def kv_shift(dy, dz):
    return [
        (kv_index(y, z, half), kv_index(y + dy, z + dz, half))
        for y in range(SIDE)
        for z in range(SIDE)
        for half in range(2)
    ]


def pb_flip(bits):
    return [(i, i ^ bits) for i in range(4)]


def far_flip(bits):
    return [(kv * 4 + pb, (kv ^ 1) * 4 + (pb ^ bits)) for kv in range(32) for pb in range(4)]


def attend_kernel(spot_ref, q_ref, *refs):
    key_parts, value_parts = refs[0:8], refs[8:16]
    o_ref, key_buf, value_buf, sems = refs[16:20]
    span_count = q_ref.shape[0] // SPAN
    head_count = q_ref.shape[1] // HEAD
    part_size = key_parts[0].shape[0]
    scale = LOG2E * HEAD ** (-0.5)
    copies = []
    for i in range(8):
        rows = pl.ds(i * part_size, part_size)
        copies.append(pltpu.make_async_copy(key_parts[i], key_buf.at[rows], sems.at[0, i]))
        copies.append(pltpu.make_async_copy(value_parts[i], value_buf.at[rows], sems.at[1, i]))
    for copy in copies:
        copy.start()
    for copy in copies:
        copy.wait()

    def one_span(span, carry):
        key_spot = spot_ref[0, span]
        value_spot = spot_ref[1, span]
        rows = pl.ds(pl.multiple_of(span * SPAN, SPAN), SPAN)
        for head in range(head_count):
            cols = slice(head * HEAD, (head + 1) * HEAD)
            scores = lax.dot_general(
                q_ref[rows, cols],
                key_buf[key_spot, :, cols],
                (((1,), (1,)), ((), ())),
                preferred_element_type=jnp.float32,
            )
            row_top = jnp.max(scores, axis=-1, keepdims=True)
            exponent = jnp.exp2((scores - row_top) * scale)
            total = jnp.sum(exponent, axis=-1, keepdims=True)
            result = jnp.dot(
                exponent.astype(jnp.bfloat16),
                value_buf[value_spot, :, cols],
                preferred_element_type=jnp.float32,
            )
            o_ref[rows, cols] = (result / total).astype(jnp.bfloat16)
        return carry

    lax.fori_loop(0, span_count, one_span, 0, unroll=2)


def attend(spots, queries, key_parts, value_parts, group):
    tok_rows = queries.shape[0]
    part_size, key_count, width = key_parts[0].shape
    flops = 4 * tok_rows * key_count * width
    return pl.pallas_call(
        attend_kernel,
        out_shape=jax.ShapeDtypeStruct((tok_rows, width), jnp.bfloat16),
        grid_spec=pltpu.PrefetchScalarGridSpec(
            num_scalar_prefetch=1,
            grid=(1,),
            in_specs=[pl.BlockSpec((tok_rows, width), lambda i, s: (0, group))]
            + [pl.BlockSpec(memory_space=pl.ANY)] * 16,
            out_specs=pl.BlockSpec((tok_rows, width), lambda i, s: (0, 0)),
            scratch_shapes=[
                pltpu.VMEM((8 * part_size, key_count, width), jnp.bfloat16),
                pltpu.VMEM((8 * part_size, key_count, width), jnp.bfloat16),
                pltpu.SemaphoreType.DMA((2, 8)),
            ],
        ),
        compiler_params=pltpu.CompilerParams(vmem_limit_bytes=32 << 20),
        cost_estimate=pl.CostEstimate(
            flops=flops * 4, bytes_accessed=20 << 20, transcendentals=0
        ),
        name="attend",
    )(spots, queries, *key_parts, *value_parts)


def line_gather(block, plus, minus):
    half = block.shape[1] // 2
    up = lax.ppermute(block, "kv", minus)
    down = lax.ppermute(block, "kv", plus)
    first = lax.ppermute(up[:, :half], "kv", minus)
    second = lax.ppermute(down[:, half:], "kv", plus)
    return [block, up, jnp.concatenate([first, second], axis=1), down]


def spread(low, high, plus, minus):
    up_low = lax.ppermute(low, "kv", minus)
    down_high = lax.ppermute(high, "kv", plus)
    up_high = lax.ppermute(high, "kv", minus)
    down_low = lax.ppermute(low, "kv", plus)
    far_low = lax.ppermute(up_low, "kv", minus)
    far_high = lax.ppermute(down_high, "kv", plus)
    return [low, high, up_low, up_high, far_low, far_high, down_low, down_high]


def on_device(queries, cached_keys, cached_values, block_map, out_weight, hidden):
    tok_rows, feat_width = queries.shape
    width = feat_width // GROUPS
    me = lax.axis_index("kv")
    pb = lax.axis_index("pb")
    targets = block_map[:, 0]
    step_y = (targets // 8 - me // 8) % SIDE
    step_z = (targets // 2 - me // 2) % SIDE
    step_h = (targets + me) % 2
    spots = jnp.stack([step_y * 8 + step_z * 2 + step_h, step_z * 8 + step_y * 2 + step_h])

    swap = [(i, i ^ 1) for i in range(32)]
    y_plus, y_minus = kv_shift(1, 0), kv_shift(-1, 0)
    z_plus, z_minus = kv_shift(0, 1), kv_shift(0, -1)

    other_keys = lax.ppermute(cached_keys, "kv", swap)
    other_values = lax.ppermute(cached_values, "kv", swap)
    own_k = line_gather(cached_keys, z_plus, z_minus)
    own_v = line_gather(cached_values, y_plus, y_minus)
    oth_k = line_gather(other_keys, z_plus, z_minus)
    oth_v = line_gather(other_values, y_plus, y_minus)

    def columns(q):
        return lax.dynamic_slice_in_dim(out_weight, q * feat_width, feat_width, 1)

    mid = feat_width // 2
    weight_mine = columns(pb)
    weight_core = lax.ppermute(columns(pb ^ 1), "pb", pb_flip(1))
    send2, send3 = columns(pb ^ 2), columns(pb ^ 3)
    weight_near = jnp.concatenate(
        [
            lax.ppermute(send2[:mid], "pb", pb_flip(2)),
            lax.ppermute(send2[mid:], ("kv", "pb"), far_flip(2)),
        ]
    )
    weight_cross = jnp.concatenate(
        [
            lax.ppermute(send3[:mid], "pb", pb_flip(3)),
            lax.ppermute(send3[mid:], ("kv", "pb"), far_flip(3)),
        ]
    )

    total = hidden.astype(jnp.float32)
    for group in range(GROUPS):
        cols = slice(group * width, (group + 1) * width)

        def pick(own, oth, steps):
            return jnp.concatenate(
                [part[:, :, cols] for s in steps for part in (own[s], oth[s])], axis=0
            )

        key_parts = spread(pick(own_k, oth_k, (0, 1)), pick(own_k, oth_k, (2, 3)), y_plus, y_minus)
        value_parts = spread(pick(own_v, oth_v, (0, 1)), pick(own_v, oth_v, (2, 3)), z_plus, z_minus)
        mine = attend(spots, queries, key_parts, value_parts, group)
        core = lax.ppermute(mine, "pb", pb_flip(1))
        near = lax.ppermute(mine, "pb", pb_flip(2))
        cross = lax.ppermute(near, "pb", pb_flip(1))
        together = jnp.concatenate([mine, core, near, cross], axis=1)
        weights = jnp.concatenate(
            [weight_mine[cols], weight_core[cols], weight_near[cols], weight_cross[cols]]
        )
        total = total + jnp.dot(together, weights, preferred_element_type=jnp.float32)
    return total.astype(jnp.bfloat16)


def solution(mesh):
    placed = (
        P("kv", "pb"),
        P("kv", None, "pb"),
        P("kv", None, "pb"),
        P("kv", None),
        P("pb", None),
        P("kv", "pb"),
    )
    return jax.shard_map(
        on_device, mesh=mesh, in_specs=placed, out_specs=P("kv", "pb"), check_vma=False
    )
```

```python
import functools

import jax
import jax.numpy as jnp
from jax import lax
from jax.experimental import pallas as pl
from jax.experimental.pallas import tpu as pltpu
from jax.sharding import PartitionSpec as P


HEAD = 128
SPAN = 64
LOG2E = 1.4426950408889634
PLANES = [[i * 2 + half for i in range(16)] for half in range(2)]
SIDE = 4
JOINT_A, RING_A, RING_B, JOINT_B = (0, 1), (2, 3), (4, 5), (6, 7)


def pb_flip(bits):
    return [(i, i ^ bits) for i in range(4)]


def far_flip(bits):
    return [(kv * 4 + pb, (kv ^ 1) * 4 + (pb ^ bits)) for kv in range(32) for pb in range(4)]


def kv_index(y, z, half):
    return ((y % SIDE) * SIDE + z % SIDE) * 2 + half


def kv_shift(dy, dz):
    return [
        (kv_index(y, z, half), kv_index(y + dy, z + dz, half))
        for y in range(SIDE)
        for z in range(SIDE)
        for half in range(2)
    ]


def attend_kernel(first_col, part_count, spot_ref, q_hbm, *refs):
    key_parts, value_parts = refs[:part_count], refs[part_count : 2 * part_count]
    o_ref, q_buf, k_buf, v_buf, sems, q_sem = refs[2 * part_count :]
    tok_rows, width = o_ref.shape
    span_count = tok_rows // SPAN
    head_count = width // HEAD
    scale = LOG2E * HEAD ** (-0.5)
    at_once = max(1, 8 // head_count)
    while span_count % at_once:
        at_once -= 1

    q_copy = pltpu.make_async_copy(q_hbm.at[:, pl.ds(first_col, width)], q_buf, q_sem)
    q_copy.start()

    def fetch(parts, held, side, span):
        for i, part in enumerate(parts):

            @pl.when(spot_ref[2 * side, span] == i)
            def _():
                pltpu.make_async_copy(
                    part.at[spot_ref[2 * side + 1, span]], held.at[span], sems.at[side, span]
                ).start()

    def start_span(span, carry):
        fetch(key_parts, k_buf, 0, span)
        fetch(value_parts, v_buf, 1, span)
        return carry

    lax.fori_loop(0, span_count, start_span, 0)
    q_copy.wait()

    def some_spans(step, carry):
        units = []
        for near in range(at_once):
            span = step * at_once + near
            pltpu.make_async_copy(key_parts[0].at[0], k_buf.at[span], sems.at[0, span]).wait()
            pltpu.make_async_copy(value_parts[0].at[0], v_buf.at[span], sems.at[1, span]).wait()
            rows = pl.ds(pl.multiple_of(span * SPAN, SPAN), SPAN)
            for head in range(head_count):
                units.append((span, rows, slice(head * HEAD, (head + 1) * HEAD)))
        scores = [
            lax.dot_general(
                q_buf[rows, cols],
                k_buf[span, :, cols],
                (((1,), (1,)), ((), ())),
                preferred_element_type=jnp.float32,
            )
            for span, rows, cols in units
        ]
        tops = [jnp.max(part, axis=-1, keepdims=True) for part in scores]
        exponents = [jnp.exp2((part - top) * scale) for part, top in zip(scores, tops)]
        totals = [jnp.sum(part, axis=-1, keepdims=True) for part in exponents]
        results = [
            jnp.dot(
                part.astype(jnp.bfloat16),
                v_buf[span, :, cols],
                preferred_element_type=jnp.float32,
            )
            for part, (span, rows, cols) in zip(exponents, units)
        ]
        for result, total, (span, rows, cols) in zip(results, totals, units):
            o_ref[rows, cols] = (result / total).astype(jnp.bfloat16)
        return carry

    lax.fori_loop(0, span_count // at_once, some_spans, 0)


def attend(spots, queries, first_col, key_parts, value_parts):
    tok_rows = queries.shape[0]
    span_count = tok_rows // SPAN
    key_count, width = key_parts[0].shape[1:]
    flops = 4 * tok_rows * key_count * width
    held = pltpu.VMEM((span_count, key_count, width), jnp.bfloat16)
    return pl.pallas_call(
        functools.partial(attend_kernel, first_col, len(key_parts)),
        out_shape=jax.ShapeDtypeStruct((tok_rows, width), jnp.bfloat16),
        grid_spec=pltpu.PrefetchScalarGridSpec(
            num_scalar_prefetch=1,
            grid=(1,),
            in_specs=[pl.BlockSpec(memory_space=pl.ANY)] * (1 + 2 * len(key_parts)),
            out_specs=pl.BlockSpec((tok_rows, width), lambda i, s: (0, 0)),
            scratch_shapes=[
                pltpu.VMEM((tok_rows, width), jnp.bfloat16),
                held,
                held,
                pltpu.SemaphoreType.DMA((2, span_count)),
                pltpu.SemaphoreType.DMA,
            ],
        ),
        compiler_params=pltpu.CompilerParams(vmem_limit_bytes=60 << 20),
        cost_estimate=pl.CostEstimate(
            flops=flops, bytes_accessed=20 << 20, transcendentals=0
        ),
        name="attend",
    )(spots, queries, *key_parts, *value_parts)


def project_kernel(base_ref, *refs):
    count = len(refs) // 2
    total = base_ref[...].astype(jnp.float32)
    for i in range(count):
        total += jnp.dot(refs[i][...], refs[count + i][...], preferred_element_type=jnp.float32)
    refs[-1][...] = total.astype(refs[-1].dtype)


def project(base, pairs, out_type):
    tok_rows, out_width = base.shape
    rows = tok_rows // 6
    features = [part for part, _, _ in pairs]
    weights = [part for _, part, _ in pairs]
    wide = pl.BlockSpec((rows, out_width), lambda i: (i, 0))

    def held(width, place):
        return pl.BlockSpec((width, out_width), lambda i: (place, 0))

    depth = sum(part.shape[1] for part in features)
    return pl.pallas_call(
        project_kernel,
        out_shape=jax.ShapeDtypeStruct((tok_rows, out_width), out_type),
        grid=(6,),
        in_specs=[wide]
        + [pl.BlockSpec((rows, part.shape[1]), lambda i: (i, 0)) for part in features]
        + [held(part.shape[1], place) for part, _, place in pairs],
        out_specs=wide,
        compiler_params=pltpu.CompilerParams(vmem_limit_bytes=40 << 20),
        cost_estimate=pl.CostEstimate(
            flops=2 * tok_rows * depth * out_width, bytes_accessed=20 << 20, transcendentals=0
        ),
    )(base, *features, *weights)


def near_ring(block, plus, minus):
    up = lax.ppermute(block, "kv", minus)
    down = lax.ppermute(block, "kv", plus)
    far = lax.ppermute(block, "kv", twice(minus))
    return jnp.concatenate([block, up, far, down])


def twice(steps):
    following = dict(steps)
    return [(source, following[target]) for source, target in steps]


def both_ways(line, plus, minus):
    return lax.ppermute(line, "kv", minus), lax.ppermute(line, "kv", plus)


def pass_on(up, down, plus, minus):
    half = up.shape[0] // 2
    first = lax.ppermute(up[:half], "kv", minus)
    second = lax.ppermute(down[half:], "kv", plus)
    return first, second


def plane_gather(payload):
    return lax.all_gather(payload, "kv", axis=0, tiled=True, axis_index_groups=PLANES)


def exchange_weights(columns, pb, mid):
    core = lax.ppermute(columns(pb ^ 1), "pb", pb_flip(1))
    send2, send3 = columns(pb ^ 2), columns(pb ^ 3)
    near = [
        lax.ppermute(send2[:mid], "pb", pb_flip(2)),
        lax.ppermute(send2[mid:], ("kv", "pb"), far_flip(2)),
    ]
    cross = [
        lax.ppermute(send3[:mid], "pb", pb_flip(3)),
        lax.ppermute(send3[mid:], ("kv", "pb"), far_flip(3)),
    ]
    return core, near, cross


def on_device(queries, cached_keys, cached_values, block_map, out_weight, hidden):
    feat_width = queries.shape[1]
    me = lax.axis_index("kv")
    pb = lax.axis_index("pb")
    targets = block_map[:, 0]
    place, is_other = targets // 2, (targets + me) % 2
    step_y = (targets // 8 - me // 8) % SIDE
    step_z = (targets // 2 - me // 2) % SIDE
    joint_spot = place * 4 + is_other * 2
    whole = jnp.zeros_like(targets)
    joint_spots = jnp.stack([whole, joint_spot, whole, joint_spot + 1])

    def ring_part(far_step, near_step):
        flat = far_step * 8 + near_step * 2 + is_other
        part = jnp.where(far_step < 2, far_step, jnp.where(far_step == 3, 4, 2 + near_step // 2))
        return part, jnp.where(far_step == 2, flat % 4, flat % 8)

    ring_spots = jnp.stack([*ring_part(step_y, step_z), *ring_part(step_z, step_y)])
    swap = [(i, i ^ 1) for i in range(32)]
    y_plus, y_minus = kv_shift(1, 0), kv_shift(-1, 0)
    z_plus, z_minus = kv_shift(0, 1), kv_shift(0, -1)

    def cols_of(heads):
        return slice(heads[0] * HEAD, (heads[-1] + 1) * HEAD)

    own_both = jnp.concatenate([cached_keys, cached_values])

    def swapped(heads):
        own = own_both[:, :, cols_of(heads)]
        return jnp.concatenate([own, lax.ppermute(own, "kv", swap)])

    both_a = swapped(JOINT_A)
    ring_heads = RING_A + RING_B
    both_r = swapped(ring_heads)
    both_late = swapped(JOINT_B)
    y_ways, z_ways = (y_plus, y_minus), (z_plus, z_minus)
    key_line = near_ring(both_r[0::2], *z_ways)
    value_line = near_ring(both_r[1::2], *y_ways)
    out_weight, key_line, value_line = lax.optimization_barrier((out_weight, key_line, value_line))

    def columns(q):
        return lax.dynamic_slice_in_dim(out_weight, q * feat_width, feat_width, 1)

    mid = feat_width // 2
    weight_mine = columns(pb)
    weight_core, weight_near, weight_cross = exchange_weights(columns, pb, mid)

    def gather_heads(heads, mine):
        width = mine.shape[1]
        place, half_place = heads[0] * HEAD // width, heads[0] * HEAD % mid // width
        half = heads[0] * HEAD // mid
        core = lax.ppermute(mine, "pb", pb_flip(1))
        near = lax.ppermute(mine, "pb", pb_flip(2))
        cross = lax.ppermute(near, "pb", pb_flip(1))
        return [
            (mine, weight_mine, place),
            (core, weight_core, place),
            (near, weight_near[half], half_place),
            (cross, weight_cross[half], half_place),
        ]

    def by_joint(payload, heads):
        joint = plane_gather(payload)
        return attend(joint_spots, queries, heads[0] * HEAD, [joint], [joint])

    def sides(heads):
        first = heads[0] * HEAD - ring_heads[0] * HEAD
        cols = slice(first, first + len(heads) * HEAD)
        keys, values = key_line[:, :, cols], value_line[:, :, cols]
        return keys, both_ways(keys, *y_ways), values, both_ways(values, *z_ways)

    def by_ring(parts, heads):
        keys, key_sides, values, value_sides = parts
        key_far = pass_on(*key_sides, *y_ways)
        value_far = pass_on(*value_sides, *z_ways)
        keys = [keys, key_sides[0], *key_far, key_sides[1]]
        values = [values, value_sides[0], *value_far, value_sides[1]]
        return attend(ring_spots, queries, heads[0] * HEAD, keys, values)

    sides_a, sides_b = sides(RING_A), sides(RING_B)
    joint_a = gather_heads(JOINT_A, by_joint(both_a, JOINT_A))
    ring_a = gather_heads(RING_A, by_ring(sides_a, RING_A))
    ring_b = gather_heads(RING_B, by_ring(sides_b, RING_B))
    joint_b = gather_heads(JOINT_B, by_joint(both_late, JOINT_B))
    total = project(hidden, joint_a + ring_a, jnp.float32)
    total = project(total, ring_b, jnp.float32)
    return project(total, joint_b, jnp.bfloat16)


def solution(mesh):
    placed = (
        P("kv", "pb"),
        P("kv", None, "pb"),
        P("kv", None, "pb"),
        P("kv", None),
        P("pb", None),
        P("kv", "pb"),
    )
    return jax.shard_map(
        on_device, mesh=mesh, in_specs=placed, out_specs=P("kv", "pb"), check_vma=False
    )
```

```python
import functools

import jax
import jax.numpy as jnp
from jax import lax
from jax.experimental import pallas as pl
from jax.experimental.pallas import tpu as pltpu
from jax.sharding import PartitionSpec as P


HEAD = 128
SPAN = 64
LOG2E = 1.4426950408889634
PLANES = [[i * 2 + half for i in range(16)] for half in range(2)]
SIDE = 4
JOINT_A, RING_A, RING_B, JOINT_B = (0, 1), (2, 3), (4, 5), (6, 7)


def pb_flip(bits):
    return [(i, i ^ bits) for i in range(4)]


def far_flip(bits):
    return [(kv * 4 + pb, (kv ^ 1) * 4 + (pb ^ bits)) for kv in range(32) for pb in range(4)]


def kv_index(y, z, half):
    return ((y % SIDE) * SIDE + z % SIDE) * 2 + half


def kv_shift(dy, dz):
    return [
        (kv_index(y, z, half), kv_index(y + dy, z + dz, half))
        for y in range(SIDE)
        for z in range(SIDE)
        for half in range(2)
    ]


def attend_kernel(first_col, part_count, spot_ref, q_hbm, *refs):
    key_parts, value_parts = refs[:part_count], refs[part_count : 2 * part_count]
    o_ref, q_buf, k_buf, v_buf, sems, q_sem = refs[2 * part_count :]
    tok_rows, width = o_ref.shape
    span_count = tok_rows // SPAN
    head_count = width // HEAD
    scale = LOG2E * HEAD ** (-0.5)
    at_once = max(1, 8 // head_count)
    while span_count % at_once:
        at_once -= 1

    q_copy = pltpu.make_async_copy(q_hbm.at[:, pl.ds(first_col, width)], q_buf, q_sem)
    q_copy.start()

    def fetch(parts, held, side, span):
        for i, part in enumerate(parts):

            @pl.when(spot_ref[2 * side, span] == i)
            def _():
                pltpu.make_async_copy(
                    part.at[spot_ref[2 * side + 1, span]], held.at[span], sems.at[side, span]
                ).start()

    def start_span(span, carry):
        fetch(key_parts, k_buf, 0, span)
        fetch(value_parts, v_buf, 1, span)
        return carry

    lax.fori_loop(0, span_count, start_span, 0)
    q_copy.wait()

    def some_spans(step, carry):
        units = []
        for near in range(at_once):
            span = step * at_once + near
            pltpu.make_async_copy(key_parts[0].at[0], k_buf.at[span], sems.at[0, span]).wait()
            pltpu.make_async_copy(value_parts[0].at[0], v_buf.at[span], sems.at[1, span]).wait()
            rows = pl.ds(pl.multiple_of(span * SPAN, SPAN), SPAN)
            for head in range(head_count):
                units.append((span, rows, slice(head * HEAD, (head + 1) * HEAD)))
        scores = [
            lax.dot_general(
                q_buf[rows, cols],
                k_buf[span, :, cols],
                (((1,), (1,)), ((), ())),
                preferred_element_type=jnp.float32,
            )
            for span, rows, cols in units
        ]
        tops = [jnp.max(part, axis=-1, keepdims=True) for part in scores]
        exponents = [jnp.exp2((part - top) * scale) for part, top in zip(scores, tops)]
        totals = [jnp.sum(part, axis=-1, keepdims=True) for part in exponents]
        results = [
            jnp.dot(
                part.astype(jnp.bfloat16),
                v_buf[span, :, cols],
                preferred_element_type=jnp.float32,
            )
            for part, (span, rows, cols) in zip(exponents, units)
        ]
        for result, total, (span, rows, cols) in zip(results, totals, units):
            o_ref[rows, cols] = (result / total).astype(jnp.bfloat16)
        return carry

    lax.fori_loop(0, span_count // at_once, some_spans, 0)


def attend(spots, queries, first_col, key_parts, value_parts):
    tok_rows = queries.shape[0]
    span_count = tok_rows // SPAN
    key_count, width = key_parts[0].shape[1:]
    flops = 4 * tok_rows * key_count * width
    held = pltpu.VMEM((span_count, key_count, width), jnp.bfloat16)
    return pl.pallas_call(
        functools.partial(attend_kernel, first_col, len(key_parts)),
        out_shape=jax.ShapeDtypeStruct((tok_rows, width), jnp.bfloat16),
        grid_spec=pltpu.PrefetchScalarGridSpec(
            num_scalar_prefetch=1,
            grid=(1,),
            in_specs=[pl.BlockSpec(memory_space=pl.ANY)] * (1 + 2 * len(key_parts)),
            out_specs=pl.BlockSpec((tok_rows, width), lambda i, s: (0, 0)),
            scratch_shapes=[
                pltpu.VMEM((tok_rows, width), jnp.bfloat16),
                held,
                held,
                pltpu.SemaphoreType.DMA((2, span_count)),
                pltpu.SemaphoreType.DMA,
            ],
        ),
        compiler_params=pltpu.CompilerParams(vmem_limit_bytes=63 << 20),
        cost_estimate=pl.CostEstimate(
            flops=flops, bytes_accessed=20 << 20, transcendentals=0
        ),
        name="attend",
    )(spots, queries, *key_parts, *value_parts)


def project_kernel(base_ref, *refs):
    count = len(refs) // 2
    total = base_ref[...].astype(jnp.float32)
    for i in range(count):
        total += jnp.dot(refs[i][...], refs[count + i][...], preferred_element_type=jnp.float32)
    refs[-1][...] = total.astype(refs[-1].dtype)


def project(base, pairs, out_type):
    tok_rows, out_width = base.shape
    rows = tok_rows // 6
    features = [part for part, _, _ in pairs]
    weights = [part for _, part, _ in pairs]
    wide = pl.BlockSpec((rows, out_width), lambda i: (i, 0))

    def held(width, place):
        return pl.BlockSpec((width, out_width), lambda i: (place, 0))

    depth = sum(part.shape[1] for part in features)
    return pl.pallas_call(
        project_kernel,
        out_shape=jax.ShapeDtypeStruct((tok_rows, out_width), out_type),
        grid=(6,),
        in_specs=[wide]
        + [pl.BlockSpec((rows, part.shape[1]), lambda i: (i, 0)) for part in features]
        + [held(part.shape[1], place) for part, _, place in pairs],
        out_specs=wide,
        compiler_params=pltpu.CompilerParams(vmem_limit_bytes=63 << 20),
        cost_estimate=pl.CostEstimate(
            flops=2 * tok_rows * depth * out_width, bytes_accessed=20 << 20, transcendentals=0
        ),
    )(base, *features, *weights)


def near_ring(block, plus, minus):
    up = lax.ppermute(block, "kv", minus)
    down = lax.ppermute(block, "kv", plus)
    far = lax.ppermute(block, "kv", twice(minus))
    return jnp.concatenate([block, up, far, down])


def twice(steps):
    following = dict(steps)
    return [(source, following[target]) for source, target in steps]


def both_ways(line, plus, minus):
    return lax.ppermute(line, "kv", minus), lax.ppermute(line, "kv", plus)


def pass_on(up, down, plus, minus):
    half = up.shape[0] // 2
    first = lax.ppermute(up[:half], "kv", minus)
    second = lax.ppermute(down[half:], "kv", plus)
    return first, second


def plane_gather(payload):
    return lax.all_gather(payload, "kv", axis=0, tiled=True, axis_index_groups=PLANES)


def exchange_weights(columns, pb, mid):
    core = lax.ppermute(columns(pb ^ 1), "pb", pb_flip(1))
    send2, send3 = columns(pb ^ 2), columns(pb ^ 3)
    near = [
        lax.ppermute(send2[:mid], "pb", pb_flip(2)),
        lax.ppermute(send2[mid:], ("kv", "pb"), far_flip(2)),
    ]
    cross = [
        lax.ppermute(send3[:mid], "pb", pb_flip(3)),
        lax.ppermute(send3[mid:], ("kv", "pb"), far_flip(3)),
    ]
    return core, near, cross


def on_device(queries, cached_keys, cached_values, block_map, out_weight, hidden):
    feat_width = queries.shape[1]
    me = lax.axis_index("kv")
    pb = lax.axis_index("pb")
    targets = block_map[:, 0]
    place, is_other = targets // 2, (targets + me) % 2
    step_y = (targets // 8 - me // 8) % SIDE
    step_z = (targets // 2 - me // 2) % SIDE
    joint_spot = place * 4 + is_other * 2
    whole = jnp.zeros_like(targets)
    joint_spots = jnp.stack([whole, joint_spot, whole, joint_spot + 1])

    def ring_part(far_step, near_step):
        flat = far_step * 8 + near_step * 2 + is_other
        part = jnp.where(far_step < 2, far_step, jnp.where(far_step == 3, 4, 2 + near_step // 2))
        return part, jnp.where(far_step == 2, flat % 4, flat % 8)

    ring_spots = jnp.stack([*ring_part(step_y, step_z), *ring_part(step_z, step_y)])
    swap = [(i, i ^ 1) for i in range(32)]
    y_plus, y_minus = kv_shift(1, 0), kv_shift(-1, 0)
    z_plus, z_minus = kv_shift(0, 1), kv_shift(0, -1)

    def cols_of(heads):
        return slice(heads[0] * HEAD, (heads[-1] + 1) * HEAD)

    own_both = jnp.concatenate([cached_keys, cached_values])

    def swapped(heads):
        own = own_both[:, :, cols_of(heads)]
        return jnp.concatenate([own, lax.ppermute(own, "kv", swap)])

    both_a = swapped(JOINT_A)
    ring_heads = RING_A + RING_B
    both_r = swapped(ring_heads)
    both_late = swapped(JOINT_B)
    y_ways, z_ways = (y_plus, y_minus), (z_plus, z_minus)
    key_line = near_ring(both_r[0::2], *z_ways)
    value_line = near_ring(both_r[1::2], *y_ways)
    out_weight, key_line, value_line = lax.optimization_barrier((out_weight, key_line, value_line))

    def columns(q):
        return lax.dynamic_slice_in_dim(out_weight, q * feat_width, feat_width, 1)

    mid = feat_width // 2
    weight_mine = columns(pb)
    weight_core, weight_near, weight_cross = exchange_weights(columns, pb, mid)

    def gather_heads(heads, mine):
        width = mine.shape[1]
        place, half_place = heads[0] * HEAD // width, heads[0] * HEAD % mid // width
        half = heads[0] * HEAD // mid
        core = lax.ppermute(mine, "pb", pb_flip(1))
        near = lax.ppermute(mine, "pb", pb_flip(2))
        cross = lax.ppermute(near, "pb", pb_flip(1))
        return [
            (mine, weight_mine, place),
            (core, weight_core, place),
            (near, weight_near[half], half_place),
            (cross, weight_cross[half], half_place),
        ]

    def by_joint(payload, heads):
        joint = plane_gather(payload)
        return attend(joint_spots, queries, heads[0] * HEAD, [joint], [joint])

    def sides(heads):
        first = heads[0] * HEAD - ring_heads[0] * HEAD
        cols = slice(first, first + len(heads) * HEAD)
        keys, values = key_line[:, :, cols], value_line[:, :, cols]
        return keys, both_ways(keys, *y_ways), values, both_ways(values, *z_ways)

    def by_ring(parts, heads):
        keys, key_sides, values, value_sides = parts
        key_far = pass_on(*key_sides, *y_ways)
        value_far = pass_on(*value_sides, *z_ways)
        keys = [keys, key_sides[0], *key_far, key_sides[1]]
        values = [values, value_sides[0], *value_far, value_sides[1]]
        return attend(ring_spots, queries, heads[0] * HEAD, keys, values)

    sides_a, sides_b = sides(RING_A), sides(RING_B)
    joint_a = gather_heads(JOINT_A, by_joint(both_a, JOINT_A))
    ring_a = gather_heads(RING_A, by_ring(sides_a, RING_A))
    ring_b = gather_heads(RING_B, by_ring(sides_b, RING_B))
    joint_b = gather_heads(JOINT_B, by_joint(both_late, JOINT_B))
    total = project(hidden, joint_a + ring_a, jnp.float32)
    total = project(total, ring_b + joint_b[:2], jnp.float32)
    return project(total, joint_b[2:], jnp.bfloat16)


def solution(mesh):
    placed = (
        P("kv", "pb"),
        P("kv", None, "pb"),
        P("kv", None, "pb"),
        P("kv", None),
        P("pb", None),
        P("kv", "pb"),
    )
    return jax.shard_map(
        on_device, mesh=mesh, in_specs=placed, out_specs=P("kv", "pb"), check_vma=False
    )
```
